256 devices in a mesh: dp: 2 (over core), width: 4 (over x), vocab: 32 (over z, y).
Axes of the slice: x: 4, y: 4, z: 8, core: 2. Of those that a mesh axis runs over, the one named last changes fastest.
Arguments:
- hidden: bfloat16 [1024, 8192], P('dp', 'width'), may hold values from -68 to 68
- head: bfloat16 [8192, 2, 32064], P('width', 'dp', 'vocab'), may hold values from -0.25 to 0.25
- teacher: bfloat16 [1024, 2, 32064], P('dp', None, 'vocab'), may hold values from -180 to 180
Outputs:
- divergence: float32 [1024], P('dp')
- grad_head: bfloat16 [8192, 2, 32064], P('width', 'dp', 'vocab')
- grad_hidden: bfloat16 [1024, 8192], P('dp', 'width')
The draws below stay inside these ranges and needn't reach their ends.
All inputs are finite; a program needn't handle non-finite values.
Results may differ from the reference program's by a relative error of at most 0.0052.
Values may be sent and summed in bfloat16 or wider, within the bound.
A program may use at most 128 MiB of HBM per device.

```python
import jax
import jax.numpy as jnp

D = 8192
VOCAB = 64128
TOKENS = 1024
N_DP = 2


def draw_hidden(key, part):
    first = jax.random.fold_in(key, 0)
    values = jnp.clip(jax.random.normal(first, (TOKENS, D), jnp.float32), -6.0, 6.0)
    return values.astype(jnp.bfloat16)


def draw_teacher(key, part):
    first = jax.random.fold_in(key, 0)
    shape = (TOKENS, N_DP, VOCAB // N_DP)
    values = jnp.clip(jax.random.normal(first, shape, jnp.float32) * 3.0, -36.0, 36.0)
    return values.astype(jnp.bfloat16)


def block_levels(stream_key, extent, cuts, low, largest):
    gain, own = 1.0, jax.random.fold_in(stream_key, 6)
    for position, blocks in cuts:
        heights = jnp.exp(jax.random.uniform(jax.random.fold_in(own, position), (blocks,), jnp.float32, low / len(cuts), largest / len(cuts)))
        gain = gain * jnp.repeat(heights, extent[position] // blocks).reshape([-1 if axis == position else 1 for axis in range(len(extent))])
    return gain


def noise(key, shape, scale, bound, shards=(), dtype=jnp.bfloat16):
    result = scale * jax.random.normal(key, shape, jnp.float32)
    if shards:
        result = result * block_levels(key, shape, shards, -0.22, 0.18)
    return jnp.clip(result, -bound, bound).astype(dtype)


def setup_inputs(seed: int = 0) -> dict:
    seeds = jax.random.split(jax.random.key(seed), 4)
    hidden = draw_hidden(jax.random.fold_in(seeds[3], 71), 0)
    head = noise(seeds[1], (D, N_DP, VOCAB // N_DP), (D // 16) ** -0.5, 0.25, ((0, 4), (1, 2), (2, 32)))
    teacher = draw_teacher(jax.random.fold_in(seeds[3], 71), 0)
    return {"hidden": hidden, "head": head, "teacher": teacher}


def reference(hidden, head, teacher):
    weight = head.reshape(D, VOCAB)
    target = teacher.reshape(TOKENS, VOCAB).astype(jnp.float32)
    student = jnp.dot(hidden, weight, preferred_element_type=jnp.float32)
    student_peak = jnp.max(student, axis=1, keepdims=True)
    student_lse = student_peak + jnp.log(jnp.sum(jnp.exp(student - student_peak), axis=1, keepdims=True))
    target_peak = jnp.max(target, axis=1, keepdims=True)
    target_lse = target_peak + jnp.log(jnp.sum(jnp.exp(target - target_peak), axis=1, keepdims=True))
    prob_student = jnp.exp(student - student_lse)
    prob_target = jnp.exp(target - target_lse)
    divergence = jnp.sum(prob_target * (target - student), axis=1) - target_lse[:, 0] + student_lse[:, 0]
    grad = (VOCAB * (prob_student - prob_target)).astype(jnp.bfloat16)
    grad_head = jnp.dot(hidden.T, grad, preferred_element_type=jnp.float32).astype(jnp.bfloat16)
    grad_head = grad_head.reshape(D, N_DP, VOCAB // N_DP)
    grad_hidden = jnp.dot(grad, weight.T, preferred_element_type=jnp.float32).astype(jnp.bfloat16)
    return divergence, grad_head, grad_hidden
```

```python
import jax
import jax.numpy as jnp
from jax import lax
from jax.experimental import pallas as pl
from jax.experimental.pallas import tpu as pltpu
from jax.sharding import PartitionSpec as P

VOCAB = 64128
MESH = pl.DeviceIdType.MESH
BF16, F32 = jnp.bfloat16, jnp.float32
WIRE = F32
NEG = -1e30
K = 2
ROWS, REAL, BULK = 1008, 1002, 1000
BLK = 128
PAIR = 2 * BLK
CHUNK = 2 * PAIR
WID = 2048
HALF = 512
TOK4 = PAIR // 4
COL8 = WID // 8

HID, TEA, STAT1, STAT2, PAIRSUM, ZSUM, ZOUT = range(7)
XRS, XAG, YRS, YAG = 7, 13, 17, 23
DIV = 27
NSEM = 28
LHID, LTEA, LOUT = range(3)


class Ring4:
    def __init__(self, axis, pos, device, send, recv):
        self.p = pos
        self.right = device(lax.rem(pos + 1, 4))
        self.left = device(lax.rem(pos + 3, 4))
        self.send, self.recv = send, recv

    def copy(self, src, dst, n, k, peer):
        return pltpu.make_async_remote_copy(
            src_ref=src, dst_ref=dst, send_sem=self.send.at[k, n], recv_sem=self.recv.at[k, n],
            device_id=peer, device_id_type=MESH,
        )


class ReduceScatter4(Ring4):
    def setup(self, k, base, src, first, second, half):
        p = self.p
        nxt, opp, prv = lax.rem(p + 1, 4), lax.rem(p + 2, 4), lax.rem(p + 3, 4)
        rows = src.shape[2]
        a, b = pl.ds(0, half), pl.ds(half, rows - half)
        self.c1 = [
            self.copy(src.at[k, opp, a], first.at[k, 0, a], base + 0, k, self.right),
            self.copy(src.at[k, opp, b], first.at[k, 1, pl.ds(0, rows - half)], base + 1, k, self.left),
        ]
        self.c2 = [
            self.copy(src.at[k, nxt, b], second.at[k, 0, b], base + 2, k, self.right),
            self.copy(src.at[k, prv, a], second.at[k, 1, a], base + 3, k, self.left),
        ]
        self.c3 = [
            self.copy(first.at[k, 0, a], second.at[k, 0, a], base + 4, k, self.right),
            self.copy(first.at[k, 1, pl.ds(0, rows - half)], second.at[k, 1, b], base + 5, k, self.left),
        ]
        self.args = (k, src, first, half, rows, nxt, prv)
        return self

    def start1(self):
        for c in self.c1:
            c.start()

    def start2(self):
        for c in self.c2:
            c.start()

    def relay(self):
        k, src, first, half, rows, nxt, prv = self.args
        self.c1[0].wait_recv()
        s = first[k, 0, 0:half].astype(F32) + src[k, nxt, 0:half].astype(F32)
        first[k, 0, 0:half] = s.astype(first.dtype)
        self.c3[0].start()
        self.c1[1].wait_recv()
        s = first[k, 1, 0 : rows - half].astype(F32) + src[k, prv, half:rows].astype(F32)
        first[k, 1, 0 : rows - half] = s.astype(first.dtype)
        self.c3[1].start()

    def finish(self):
        for c in self.c2 + self.c3:
            c.wait_recv()

    def drain(self):
        for c in self.c1 + self.c2 + self.c3:
            c.wait_send()


class AllGather4(Ring4):
    def setup(self, k, base, buf, half):
        p = self.p
        nxt, prv = lax.rem(p + 1, 4), lax.rem(p + 3, 4)
        rows = buf.shape[2]
        a, b = pl.ds(0, half), pl.ds(half, rows - half)
        self.c1 = [
            self.copy(buf.at[k, p], buf.at[k, p], base + 0, k, self.right),
            self.copy(buf.at[k, p], buf.at[k, p], base + 1, k, self.left),
        ]
        self.c2 = [
            self.copy(buf.at[k, prv, a], buf.at[k, prv, a], base + 2, k, self.right),
            self.copy(buf.at[k, nxt, b], buf.at[k, nxt, b], base + 3, k, self.left),
        ]
        return self

    def start1(self):
        for c in self.c1:
            c.start()

    def relay(self):
        self.c1[0].wait_recv()
        self.c2[0].start()
        self.c1[1].wait_recv()
        self.c2[1].start()

    def finish(self):
        for c in self.c2:
            c.wait_recv()

    def drain(self):
        for c in self.c1 + self.c2:
            c.wait_send()


def merge(tiles):
    ms = [t[0:1] for t in tiles]
    mt = [t[2:3] for t in tiles]
    top_s, top_t = ms[0], mt[0]
    for i in range(1, len(tiles)):
        top_s, top_t = jnp.maximum(top_s, ms[i]), jnp.maximum(top_t, mt[i])
    sum_s = sum_t = cross = jnp.zeros_like(top_s)
    for t, a, b in zip(tiles, ms, mt):
        fs, ft = jnp.exp(a - top_s), jnp.exp(b - top_t)
        sum_s = sum_s + t[1:2] * fs
        sum_t = sum_t + t[3:4] * ft
        cross = cross + t[4:5] * ft
    return top_s, sum_s, top_t, sum_t, cross


def kernel(
    hid_ref, head_ref, tail_ref, tea_ref, div_ref, gh_ref, ghid_ref,
    hid, head, tea, part, first, second, logit, st0, st1, st2, st3, grad, gradn,
    theirs, arrive, mine, ysrc, yfirst, ysecond, zsrc, zin, fin, gout, divs,
    send, recv, local, head_sem, out_sem,
):
    c = lax.axis_index("dp")
    w = lax.axis_index("width")
    v = lax.axis_index("vocab")
    y, z = lax.rem(v, 4), v // 4
    partner = {"dp": 1 - c}

    def x_dev(q):
        return {"width": q}

    def y_dev(q):
        return {"vocab": z * 4 + q}

    def cy(i):
        j = lax.rem(c * 4 + y + i, 8)
        return {"dp": j // 4, "vocab": z * 4 + lax.rem(j, 4)}

    def z_dev(i):
        return {"vocab": lax.rem(z + i, 8) * 4 + y}

    head_copies = [
        pltpu.make_async_copy(head_ref.at[pl.ds(0, BULK)], head.at[pl.ds(0, BULK)], head_sem.at[0]),
        pltpu.make_async_copy(tail_ref, head.at[pl.ds(BULK, ROWS - BULK)], head_sem.at[1]),
    ]
    for cp in head_copies:
        cp.start()
    hid_copies = [
        pltpu.make_async_copy(hid_ref.at[pl.ds(k * PAIR, PAIR)], hid.at[k, c], local.at[k, LHID]) for k in range(K)
    ]
    for cp in hid_copies:
        cp.start()

    barrier = pltpu.get_barrier_semaphore()
    for i in range(1, 8):
        pl.semaphore_signal(barrier, inc=1, device_id=cy(i), device_id_type=MESH)
        pl.semaphore_signal(barrier, inc=1, device_id=z_dev(i), device_id_type=MESH)
    for i in range(1, 4):
        pl.semaphore_signal(barrier, inc=1, device_id=x_dev(lax.rem(w + i, 4)), device_id_type=MESH)
    pl.semaphore_wait(barrier, 17)

    def remote(src, dst, n, k, peer):
        return pltpu.make_async_remote_copy(
            src_ref=src, dst_ref=dst, send_sem=send.at[k, n], recv_sem=recv.at[k, n],
            device_id=peer, device_id_type=MESH,
        )

    hid_sends = [remote(hid_ref.at[pl.ds(k * PAIR, PAIR)], hid.at[k, c], HID, k, partner) for k in range(K)]
    for cp in hid_sends:
        cp.start()
    holder = c == w // 2
    place = lax.rem(w, 2) * BLK

    def tea_copy(k):
        cols = pl.ds(pl.multiple_of(k * PAIR + place, BLK), BLK)
        return (
            pltpu.make_async_copy(tea_ref.at[c, :, cols], tea.at[k], local.at[k, LTEA]),
            remote(tea_ref.at[1 - c, :, cols], tea.at[k], TEA, k, partner),
        )

    tea_copies = [tea_copy(k) for k in range(K)]

    @pl.when(holder)
    def _():
        for here, there in tea_copies:
            there.start()
            here.start()

    xrs = [ReduceScatter4("width", w, x_dev, send, recv).setup(k, XRS, part, first, second, HALF) for k in range(K)]
    xag = [AllGather4("width", w, x_dev, send, recv).setup(k, XAG, grad, HALF) for k in range(K)]
    yrs = [
        ReduceScatter4("vocab", y, y_dev, send, recv).setup(k, YRS, ysrc, yfirst, ysecond, TOK4 // 2) for k in range(K)
    ]
    yag = [AllGather4("vocab", y, y_dev, send, recv).setup(k, YAG, fin, TOK4 // 2) for k in range(K)]

    def logits(k, d):
        for lo, hi in ((0, HALF), (HALF, ROWS)):
            out = lax.dot_general(
                head[lo:hi, :], hid[k, d], (((1,), (1,)), ((), ())), preferred_element_type=F32
            )
            part[k, 2 * d, lo:hi] = out[:, :BLK].astype(WIRE)
            part[k, 2 * d + 1, lo:hi] = out[:, BLK:].astype(WIRE)

    def wait_hidden(k):
        hid_copies[k].wait()
        hid_sends[k].wait_recv()

    def statistics(k):
        xrs[k].finish()

        @pl.when(holder)
        def _():
            tea_copies[k][0].wait()

        @pl.when(jnp.logical_not(holder))
        def _():
            tea_copies[k][1].wait_recv()

        x = part[k, w].astype(F32) + second[k, 0].astype(F32) + second[k, 1].astype(F32)
        row = lax.broadcasted_iota(jnp.int32, x.shape, 0)
        x = jnp.where(row < REAL, x, NEG)
        logit[k] = x
        t = tea[k].astype(F32)
        top_s = jnp.max(x, axis=0, keepdims=True)
        top_t = jnp.max(t, axis=0, keepdims=True)
        exp_t = jnp.exp(t - top_t)
        st0[k, 0:1] = top_s
        st0[k, 1:2] = jnp.sum(jnp.exp(x - top_s), axis=0, keepdims=True)
        st0[k, 2:3] = top_t
        st0[k, 3:4] = jnp.sum(exp_t, axis=0, keepdims=True)
        st0[k, 4:5] = jnp.sum(exp_t * (t - x), axis=0, keepdims=True)
        st0[k, 5:8] = jnp.zeros((3, BLK), F32)
        me = c * 4 + y
        st1[k, me] = st0[k]
        for i in range(1, 8):
            remote(st0.at[k], st1.at[k, me], STAT1, k, cy(i)).start()

    def seven(buf, k):
        return buf.at[k, pl.ds(0, 7)]

    def statistics_far(k):
        remote(seven(st1, k), seven(st1, k), STAT1, k, cy(1)).wait_recv()
        got = merge([st1[k, i] for i in range(8)])
        for i in range(5):
            st2[k, i : i + 1] = got[i]
        st2[k, 5:8] = jnp.zeros((3, BLK), F32)
        st3[k, z] = st2[k]
        for i in range(1, 8):
            remote(st2.at[k], st3.at[k, z], STAT2, k, z_dev(i)).start()

    def gradient(k):
        remote(seven(st3, k), seven(st3, k), STAT2, k, z_dev(1)).wait_recv()
        top_s, sum_s, top_t, sum_t, cross = merge([st3[k, i] for i in range(8)])
        lse_s = top_s + jnp.log(sum_s)
        lse_t = top_t + jnp.log(sum_t)
        divs[k, w] = jnp.broadcast_to(cross / sum_t - lse_t + lse_s, (8, BLK))
        g = VOCAB * (jnp.exp(logit[k] - lse_s) - jnp.exp(tea[k].astype(F32) - lse_t))
        grad[k, w] = g.astype(BF16)
        xag[k].start1()
        for i in range(1, 4):
            remote(divs.at[k, w], divs.at[k, w], DIV, k, x_dev(lax.rem(w + i, 4))).start()

    def hidden_terms(k):
        xag[k].finish()
        for d, final in ((1 - c, False), (c, True)):
            gn = jnp.concatenate([grad[k, 2 * d], grad[k, 2 * d + 1]], axis=1)
            gradn[...] = gn.T

            def tile(j, carry):
                cols = pl.ds(pl.multiple_of(j * 512, 512), 512)
                out = jnp.dot(gradn[...], head[:, cols], preferred_element_type=F32)
                if final:
                    mine[:, cols] = out
                else:
                    theirs[k, :, cols] = out.astype(BF16)
                return carry

            lax.fori_loop(0, WID // 512, tile, 0)
            if not final:
                remote(theirs.at[k], arrive.at[k], PAIRSUM, k, partner).start()

    def pair_sum(k):
        remote(theirs.at[k], arrive.at[k], PAIRSUM, k, partner).wait_recv()
        for i in range(4):
            rows = slice(i * TOK4, (i + 1) * TOK4)
            ysrc[k, i] = (mine[rows] + arrive[k, rows].astype(F32)).astype(BF16)
        yrs[k].start1()
        yrs[k].start2()

    def z_sum(k):
        yrs[k].finish()
        s = ysrc[k, y].astype(F32) + ysecond[k, 0].astype(F32) + ysecond[k, 1].astype(F32)
        s = s.astype(BF16)
        for i in range(8):
            zsrc[k, i] = s[:, i * COL8 : (i + 1) * COL8]
        zin[k, z] = zsrc[k, z]
        for i in range(1, 8):
            q = lax.rem(z + i, 8)
            remote(zsrc.at[k, q], zin.at[k, z], ZSUM, k, z_dev(i)).start()

    def my_cols():
        return pl.ds(pl.multiple_of(z * COL8, COL8), COL8)

    def z_gather(k):
        remote(seven(zin, k), seven(zin, k), ZSUM, k, z_dev(1)).wait_recv()
        s = zin[k, 0].astype(F32)
        for i in range(1, 8):
            s = s + zin[k, i].astype(F32)
        fin[k, y, :, my_cols()] = s.astype(BF16)
        mine_ref = fin.at[k, y, :, my_cols()]
        for i in range(1, 8):
            remote(mine_ref, mine_ref, ZOUT, k, z_dev(i)).start()

    def y_gather(k):
        span = fin.at[k, y, :, pl.ds(0, 7 * COL8)]
        remote(span, span, ZOUT, k, z_dev(1)).wait_recv()
        yag[k].start1()

    def put_hidden(k):
        yag[k].finish()
        for i in range(4):
            pltpu.make_async_copy(
                fin.at[k, i], ghid_ref.at[pl.ds(k * PAIR + i * TOK4, TOK4)], out_sem.at[k, i]
            ).start()

    def head_terms(js):
        for j in js:
            cols = slice(j * 256, (j + 1) * 256)
            for lo, hi in ((0, HALF), (HALF, ROWS)):
                total = None
                for k in range(K):
                    g = jnp.concatenate([grad[k, b, lo:hi] for b in range(4)], axis=1)
                    h = hid[k, :, :, cols].reshape(CHUNK, 256)
                    term = jnp.dot(g, h, preferred_element_type=F32)
                    total = term if total is None else total + term
                gout[lo:hi, cols] = total.astype(BF16)
            pltpu.make_async_copy(gout.at[:, cols], gh_ref.at[:, cols], out_sem.at[2, j]).start()

    for cp in head_copies[:0]:
        cp.wait()
    opp, own = 1 - w // 2, w // 2
    wait_hidden(0)
    for cp in head_copies:
        cp.wait()
    logits(0, opp)
    xrs[0].start1()
    logits(0, own)
    xrs[0].start2()
    wait_hidden(1)
    logits(1, opp)
    logits(1, own)
    xrs[0].relay()
    xrs[1].start1()
    xrs[1].start2()
    statistics(0)
    xrs[1].relay()
    statistics_far(0)
    gradient(0)
    statistics(1)
    xag[0].relay()
    statistics_far(1)
    hidden_terms(0)
    gradient(1)
    pair_sum(0)
    xag[1].relay()
    yrs[0].relay()
    z_sum(0)
    hidden_terms(1)
    z_gather(0)
    pair_sum(1)
    y_gather(0)
    head_terms((0, 1))
    yrs[1].relay()
    yag[0].relay()
    head_terms((2,))
    z_sum(1)
    put_hidden(0)
    head_terms((3, 4))
    z_gather(1)
    head_terms((5,))
    y_gather(1)
    head_terms((6, 7))
    yag[1].relay()
    for k in range(K):
        span3 = divs.at[k, pl.ds(0, 3)]
        remote(span3, span3, DIV, k, x_dev(lax.rem(w + 1, 4))).wait_recv()
        for i in range(2):
            div_ref[2 * k + i : 2 * k + i + 1] = divs[k, 2 * c + i, 0:1]
    put_hidden(1)

    for k in range(K):
        hid_sends[k].wait_send()
        for r in (xrs[k], xag[k], yrs[k], yag[k]):
            r.drain()
        remote(seven(st1, k), seven(st1, k), STAT1, k, cy(1)).wait_send()
        remote(seven(st3, k), seven(st3, k), STAT2, k, z_dev(1)).wait_send()
        remote(theirs.at[k], arrive.at[k], PAIRSUM, k, partner).wait_send()
        remote(seven(zin, k), seven(zin, k), ZSUM, k, z_dev(1)).wait_send()
        span = fin.at[k, y, :, pl.ds(0, 7 * COL8)]
        remote(span, span, ZOUT, k, z_dev(1)).wait_send()
        span3 = divs.at[k, pl.ds(0, 3)]
        remote(span3, span3, DIV, k, x_dev(lax.rem(w + 1, 4))).wait_send()
        for i in range(4):
            pltpu.make_async_copy(
                fin.at[k, i], ghid_ref.at[pl.ds(k * PAIR + i * TOK4, TOK4)], out_sem.at[k, i]
            ).wait()
    for j in range(8):
        cols = slice(j * 256, (j + 1) * 256)
        pltpu.make_async_copy(gout.at[:, cols], gh_ref.at[:, cols], out_sem.at[2, j]).wait()

    @pl.when(holder)
    def _():
        for _, there in tea_copies:
            there.wait_send()


def body(hidden, head, teacher):
    head_t = head.reshape(WID, REAL).T
    tail = jnp.pad(head_t[BULK:], ((0, ROWS - REAL), (0, 0)))
    teacher_t = jnp.pad(
        jnp.transpose(teacher, (1, 2, 0)), ((0, 0), (0, ROWS - REAL), (0, 0)), constant_values=NEG
    )
    any_space = pl.BlockSpec(memory_space=pl.ANY)
    vmem = pltpu.VMEM
    div, gh, ghid = pl.pallas_call(
        kernel,
        out_shape=(
            jax.ShapeDtypeStruct((4, BLK), F32),
            jax.ShapeDtypeStruct((ROWS, WID), BF16),
            jax.ShapeDtypeStruct((K * PAIR, WID), BF16),
        ),
        in_specs=[any_space] * 4,
        out_specs=(pl.BlockSpec(memory_space=pltpu.VMEM), any_space, any_space),
        scratch_shapes=[
            vmem((K, 2, PAIR, WID), BF16),
            vmem((ROWS, WID), BF16),
            vmem((K, ROWS, BLK), BF16),
            vmem((K, 4, ROWS, BLK), WIRE),
            vmem((K, 2, HALF, BLK), WIRE),
            vmem((K, 2, ROWS, BLK), WIRE),
            vmem((K, ROWS, BLK), F32),
            vmem((K, 8, BLK), F32),
            vmem((K, 8, 8, BLK), F32),
            vmem((K, 8, BLK), F32),
            vmem((K, 8, 8, BLK), F32),
            vmem((K, 4, ROWS, BLK), BF16),
            vmem((PAIR, ROWS), BF16),
            vmem((K, PAIR, WID), BF16),
            vmem((K, PAIR, WID), BF16),
            vmem((PAIR, WID), F32),
            vmem((K, 4, TOK4, WID), BF16),
            vmem((K, 2, TOK4 // 2, WID), BF16),
            vmem((K, 2, TOK4, WID), BF16),
            vmem((K, 8, TOK4, COL8), BF16),
            vmem((K, 8, TOK4, COL8), BF16),
            vmem((K, 4, TOK4, WID), BF16),
            vmem((ROWS, WID), BF16),
            vmem((K, 4, 8, BLK), F32),
            pltpu.SemaphoreType.DMA((K, NSEM)),
            pltpu.SemaphoreType.DMA((K, NSEM)),
            pltpu.SemaphoreType.DMA((K, 2)),
            pltpu.SemaphoreType.DMA((2,)),
            pltpu.SemaphoreType.DMA((3, 8)),
        ],
        compiler_params=pltpu.CompilerParams(
            collective_id=0, has_side_effects=True, vmem_limit_bytes=60 * 1024 * 1024
        ),
    )(hidden, head_t, tail, teacher_t)
    return div.reshape(K * PAIR), gh[:REAL].T.reshape(WID, 1, REAL), ghid


def solution(mesh):
    return jax.shard_map(
        body,
        mesh=mesh,
        in_specs=(P("dp", "width"), P("width", "dp", "vocab"), P("dp", None, "vocab")),
        out_specs=(P("dp"), P("width", "dp", "vocab"), P("dp", "width")),
        check_vma=False,
    )
```

```python
import jax
import jax.numpy as jnp
from jax import lax
from jax.experimental import pallas as pl
from jax.experimental.pallas import tpu as pltpu
from jax.sharding import PartitionSpec as P

VOCAB = 64128
MESH = pl.DeviceIdType.MESH
BF16, F32 = jnp.bfloat16, jnp.float32
WIRE = F32
K = 2
ROWS, REAL = 1008, 1002
BLK = 128
PAIR = 2 * BLK
CHUNK = 2 * PAIR
WID = 2048
HALF = 512
TOK4 = PAIR // 4
COL8 = WID // 8

HID, TEA, STAT1, STAT2, PAIRSUM, ZSUM, ZOUT = range(7)
XRS, XAG, YRS, YAG = 7, 13, 17, 23
DIV = 27
NSEM = 28
LHID, LTEA, LOUT = range(3)


class Ring4:
    def __init__(self, axis, pos, device, send, recv):
        self.p = pos
        self.right = device(lax.rem(pos + 1, 4))
        self.left = device(lax.rem(pos + 3, 4))
        self.send, self.recv = send, recv

    def copy(self, src, dst, n, k, peer):
        return pltpu.make_async_remote_copy(
            src_ref=src, dst_ref=dst, send_sem=self.send.at[k, n], recv_sem=self.recv.at[k, n],
            device_id=peer, device_id_type=MESH,
        )


class ReduceScatter4(Ring4):
    def setup(self, k, base, src, first, second, half):
        p = self.p
        nxt, opp, prv = lax.rem(p + 1, 4), lax.rem(p + 2, 4), lax.rem(p + 3, 4)
        rows = src.shape[2]
        a, b = pl.ds(0, half), pl.ds(half, rows - half)
        self.c1 = [
            self.copy(src.at[k, opp, a], first.at[k, 0, a], base + 0, k, self.right),
            self.copy(src.at[k, opp, b], first.at[k, 1, pl.ds(0, rows - half)], base + 1, k, self.left),
        ]
        self.c2 = [
            self.copy(src.at[k, nxt, b], second.at[k, 0, b], base + 2, k, self.right),
            self.copy(src.at[k, prv, a], second.at[k, 1, a], base + 3, k, self.left),
        ]
        self.c3 = [
            self.copy(first.at[k, 0, a], second.at[k, 0, a], base + 4, k, self.right),
            self.copy(first.at[k, 1, pl.ds(0, rows - half)], second.at[k, 1, b], base + 5, k, self.left),
        ]
        self.args = (k, src, first, half, rows, nxt, prv)
        return self

    def start1(self):
        for c in self.c1:
            c.start()

    def start2(self):
        for c in self.c2:
            c.start()

    def relay(self):
        k, src, first, half, rows, nxt, prv = self.args
        self.c1[0].wait_recv()
        s = first[k, 0, 0:half].astype(F32) + src[k, nxt, 0:half].astype(F32)
        first[k, 0, 0:half] = s.astype(first.dtype)
        self.c3[0].start()
        self.c1[1].wait_recv()
        s = first[k, 1, 0 : rows - half].astype(F32) + src[k, prv, half:rows].astype(F32)
        first[k, 1, 0 : rows - half] = s.astype(first.dtype)
        self.c3[1].start()

    def finish(self):
        for c in self.c2 + self.c3:
            c.wait_recv()

    def drain(self):
        for c in self.c1 + self.c2 + self.c3:
            c.wait_send()


class AllGather4(Ring4):
    def setup(self, k, base, buf, half):
        p = self.p
        nxt, prv = lax.rem(p + 1, 4), lax.rem(p + 3, 4)
        rows = buf.shape[2]
        a, b = pl.ds(0, half), pl.ds(half, rows - half)
        self.c1 = [
            self.copy(buf.at[k, p], buf.at[k, p], base + 0, k, self.right),
            self.copy(buf.at[k, p], buf.at[k, p], base + 1, k, self.left),
        ]
        self.c2 = [
            self.copy(buf.at[k, prv, a], buf.at[k, prv, a], base + 2, k, self.right),
            self.copy(buf.at[k, nxt, b], buf.at[k, nxt, b], base + 3, k, self.left),
        ]
        return self

    def start1(self):
        for c in self.c1:
            c.start()

    def relay(self):
        self.c1[0].wait_recv()
        self.c2[0].start()
        self.c1[1].wait_recv()
        self.c2[1].start()

    def finish(self):
        for c in self.c2:
            c.wait_recv()

    def drain(self):
        for c in self.c1 + self.c2:
            c.wait_send()


def merge(tiles):
    ms = [t[0:1] for t in tiles]
    mt = [t[2:3] for t in tiles]
    top_s, top_t = ms[0], mt[0]
    for i in range(1, len(tiles)):
        top_s, top_t = jnp.maximum(top_s, ms[i]), jnp.maximum(top_t, mt[i])
    sum_s = sum_t = cross = jnp.zeros_like(top_s)
    for t, a, b in zip(tiles, ms, mt):
        fs, ft = jnp.exp(a - top_s), jnp.exp(b - top_t)
        sum_s = sum_s + t[1:2] * fs
        sum_t = sum_t + t[3:4] * ft
        cross = cross + t[4:5] * ft
    return top_s, sum_s, top_t, sum_t, cross


def kernel(
    hid_ref, head_ref, tea_ref, div_ref, gh_ref, ghid_ref,
    hid, head, tea, part, first, second, logit, st0, st1, st2, st3, grad, gradn,
    theirs, arrive, mine, ysrc, yfirst, ysecond, zsrc, zin, fin, gout, divs,
    send, recv, local, head_sem, out_sem,
):
    c = lax.axis_index("dp")
    w = lax.axis_index("width")
    v = lax.axis_index("vocab")
    y, z = lax.rem(v, 4), v // 4
    partner = {"dp": 1 - c}

    def x_dev(q):
        return {"width": q}

    def y_dev(q):
        return {"vocab": z * 4 + q}

    def cy(i):
        j = lax.rem(c * 4 + y + i, 8)
        return {"dp": j // 4, "vocab": z * 4 + lax.rem(j, 4)}

    def z_dev(i):
        return {"vocab": lax.rem(z + i, 8) * 4 + y}

    head_copy = pltpu.make_async_copy(head_ref, head, head_sem.at[0])
    head_copy.start()
    hid_copies = [
        pltpu.make_async_copy(hid_ref.at[pl.ds(k * PAIR, PAIR)], hid.at[k, c], local.at[k, LHID]) for k in range(K)
    ]
    for cp in hid_copies:
        cp.start()

    barrier = pltpu.get_barrier_semaphore()
    for i in range(1, 8):
        pl.semaphore_signal(barrier, inc=1, device_id=cy(i), device_id_type=MESH)
        pl.semaphore_signal(barrier, inc=1, device_id=z_dev(i), device_id_type=MESH)
    for i in range(1, 4):
        pl.semaphore_signal(barrier, inc=1, device_id=x_dev(lax.rem(w + i, 4)), device_id_type=MESH)
    pl.semaphore_wait(barrier, 17)

    def remote(src, dst, n, k, peer):
        return pltpu.make_async_remote_copy(
            src_ref=src, dst_ref=dst, send_sem=send.at[k, n], recv_sem=recv.at[k, n],
            device_id=peer, device_id_type=MESH,
        )

    hid_sends = [remote(hid_ref.at[pl.ds(k * PAIR, PAIR)], hid.at[k, c], HID, k, partner) for k in range(K)]
    for cp in hid_sends:
        cp.start()
    holder = c == w // 2
    place = lax.rem(w, 2) * BLK

    def tea_copy(k):
        cols = pl.ds(pl.multiple_of(k * PAIR + place, BLK), BLK)
        return (
            pltpu.make_async_copy(tea_ref.at[c, :, cols], tea.at[k], local.at[k, LTEA]),
            remote(tea_ref.at[1 - c, :, cols], tea.at[k], TEA, k, partner),
        )

    tea_copies = [tea_copy(k) for k in range(K)]

    @pl.when(holder)
    def _():
        for here, there in tea_copies:
            there.start()
            here.start()

    xrs = [ReduceScatter4("width", w, x_dev, send, recv).setup(k, XRS, part, first, second, HALF) for k in range(K)]
    xag = [AllGather4("width", w, x_dev, send, recv).setup(k, XAG, grad, HALF) for k in range(K)]
    yrs = [
        ReduceScatter4("vocab", y, y_dev, send, recv).setup(k, YRS, ysrc, yfirst, ysecond, TOK4 // 2) for k in range(K)
    ]
    yag = [AllGather4("vocab", y, y_dev, send, recv).setup(k, YAG, fin, TOK4 // 2) for k in range(K)]

    def logits(k, d):
        for lo, hi in ((0, HALF), (HALF, REAL)):
            if hi == REAL:
                part[k, 2 * d, ROWS - 8 : ROWS] = jnp.zeros((8, BLK), WIRE)
                part[k, 2 * d + 1, ROWS - 8 : ROWS] = jnp.zeros((8, BLK), WIRE)
            out = lax.dot_general(
                head[lo:hi, :], hid[k, d], (((1,), (1,)), ((), ())), preferred_element_type=F32
            )
            part[k, 2 * d, lo:hi] = out[:, :BLK].astype(WIRE)
            part[k, 2 * d + 1, lo:hi] = out[:, BLK:].astype(WIRE)

    def wait_hidden(k):
        hid_copies[k].wait()
        hid_sends[k].wait_recv()

    def statistics(k):
        xrs[k].finish()

        @pl.when(holder)
        def _():
            tea_copies[k][0].wait()

        @pl.when(jnp.logical_not(holder))
        def _():
            tea_copies[k][1].wait_recv()

        x = part[k, w, 0:REAL] + second[k, 0, 0:REAL] + second[k, 1, 0:REAL]
        logit[k] = x
        t = tea[k].astype(F32)
        top_s = jnp.max(x, axis=0, keepdims=True)
        top_t = jnp.max(t, axis=0, keepdims=True)
        exp_t = jnp.exp(t - top_t)
        st0[k, 0:1] = top_s
        st0[k, 1:2] = jnp.sum(jnp.exp(x - top_s), axis=0, keepdims=True)
        st0[k, 2:3] = top_t
        st0[k, 3:4] = jnp.sum(exp_t, axis=0, keepdims=True)
        st0[k, 4:5] = jnp.sum(exp_t * (t - x), axis=0, keepdims=True)
        st0[k, 5:8] = jnp.zeros((3, BLK), F32)
        me = c * 4 + y
        st1[k, me] = st0[k]
        for i in range(1, 8):
            remote(st0.at[k], st1.at[k, me], STAT1, k, cy(i)).start()

    def seven(buf, k):
        return buf.at[k, pl.ds(0, 7)]

    def statistics_far(k):
        remote(seven(st1, k), seven(st1, k), STAT1, k, cy(1)).wait_recv()
        got = merge([st1[k, i] for i in range(8)])
        for i in range(5):
            st2[k, i : i + 1] = got[i]
        st2[k, 5:8] = jnp.zeros((3, BLK), F32)
        st3[k, z] = st2[k]
        for i in range(1, 8):
            remote(st2.at[k], st3.at[k, z], STAT2, k, z_dev(i)).start()

    def gradient(k):
        remote(seven(st3, k), seven(st3, k), STAT2, k, z_dev(1)).wait_recv()
        top_s, sum_s, top_t, sum_t, cross = merge([st3[k, i] for i in range(8)])
        lse_s = top_s + jnp.log(sum_s)
        lse_t = top_t + jnp.log(sum_t)
        divs[k, w] = jnp.broadcast_to(cross / sum_t - lse_t + lse_s, (8, BLK))
        g = VOCAB * (jnp.exp(logit[k] - lse_s) - jnp.exp(tea[k].astype(F32) - lse_t))
        grad[k, w, ROWS - 16 : ROWS] = jnp.zeros((16, BLK), BF16)
        grad[k, w, 0:REAL] = g.astype(BF16)
        xag[k].start1()
        for i in range(1, 4):
            remote(divs.at[k, w], divs.at[k, w], DIV, k, x_dev(lax.rem(w + i, 4))).start()

    def hidden_terms(k):
        xag[k].finish()
        for d, final in ((1 - c, False), (c, True)):
            gn = jnp.concatenate([grad[k, 2 * d], grad[k, 2 * d + 1]], axis=1)
            gradn[...] = gn.T

            def tile(j, carry):
                cols = pl.ds(pl.multiple_of(j * 512, 512), 512)
                out = jnp.dot(gradn[:, 0:REAL], head[:, cols], preferred_element_type=F32)
                if final:
                    mine[:, cols] = out
                else:
                    theirs[k, :, cols] = out.astype(BF16)
                return carry

            lax.fori_loop(0, WID // 512, tile, 0)
            if not final:
                remote(theirs.at[k], arrive.at[k], PAIRSUM, k, partner).start()

    def pair_sum(k):
        remote(theirs.at[k], arrive.at[k], PAIRSUM, k, partner).wait_recv()
        for i in range(4):
            rows = slice(i * TOK4, (i + 1) * TOK4)
            ysrc[k, i] = (mine[rows] + arrive[k, rows].astype(F32)).astype(BF16)
        yrs[k].start1()
        yrs[k].start2()

    def z_sum(k):
        yrs[k].finish()
        s = ysrc[k, y].astype(F32) + ysecond[k, 0].astype(F32) + ysecond[k, 1].astype(F32)
        s = s.astype(BF16)
        for i in range(8):
            zsrc[k, i] = s[:, i * COL8 : (i + 1) * COL8]
        zin[k, z] = zsrc[k, z]
        for i in range(1, 8):
            q = lax.rem(z + i, 8)
            remote(zsrc.at[k, q], zin.at[k, z], ZSUM, k, z_dev(i)).start()

    def my_cols():
        return pl.ds(pl.multiple_of(z * COL8, COL8), COL8)

    def z_gather(k):
        remote(seven(zin, k), seven(zin, k), ZSUM, k, z_dev(1)).wait_recv()
        s = zin[k, 0].astype(F32)
        for i in range(1, 8):
            s = s + zin[k, i].astype(F32)
        fin[k, y, :, my_cols()] = s.astype(BF16)
        mine_ref = fin.at[k, y, :, my_cols()]
        for i in range(1, 8):
            remote(mine_ref, mine_ref, ZOUT, k, z_dev(i)).start()

    def y_gather(k):
        span = fin.at[k, y, :, pl.ds(0, 7 * COL8)]
        remote(span, span, ZOUT, k, z_dev(1)).wait_recv()
        yag[k].start1()

    def put_hidden(k):
        yag[k].finish()
        for i in range(4):
            pltpu.make_async_copy(
                fin.at[k, i], ghid_ref.at[pl.ds(k * PAIR + i * TOK4, TOK4)], out_sem.at[k, i]
            ).start()

    def head_terms(js):
        for j in js:
            cols = slice(j * 256, (j + 1) * 256)
            for lo, hi in ((0, HALF), (HALF, REAL)):
                total = None
                for k in range(K):
                    g = jnp.concatenate([grad[k, b, lo:hi] for b in range(4)], axis=1)
                    h = hid[k, :, :, cols].reshape(CHUNK, 256)
                    term = jnp.dot(g, h, preferred_element_type=F32)
                    total = term if total is None else total + term
                gout[lo:hi, cols] = total.astype(BF16)
            pltpu.make_async_copy(gout.at[:, cols], gh_ref.at[:, cols], out_sem.at[2, j]).start()

    opp, own = 1 - w // 2, w // 2
    wait_hidden(0)
    head_copy.wait()
    logits(0, opp)
    xrs[0].start1()
    logits(0, own)
    xrs[0].start2()
    wait_hidden(1)
    logits(1, opp)
    logits(1, own)
    xrs[0].relay()
    xrs[1].start1()
    xrs[1].start2()
    statistics(0)
    xrs[1].relay()
    statistics_far(0)
    gradient(0)
    statistics(1)
    xag[0].relay()
    statistics_far(1)
    hidden_terms(0)
    gradient(1)
    pair_sum(0)
    xag[1].relay()
    yrs[0].relay()
    z_sum(0)
    hidden_terms(1)
    z_gather(0)
    pair_sum(1)
    y_gather(0)
    head_terms((0, 1))
    yrs[1].relay()
    yag[0].relay()
    head_terms((2,))
    z_sum(1)
    put_hidden(0)
    head_terms((3, 4))
    z_gather(1)
    head_terms((5,))
    y_gather(1)
    head_terms((6, 7))
    yag[1].relay()
    for k in range(K):
        span3 = divs.at[k, pl.ds(0, 3)]
        remote(span3, span3, DIV, k, x_dev(lax.rem(w + 1, 4))).wait_recv()
        for i in range(2):
            div_ref[2 * k + i : 2 * k + i + 1] = divs[k, 2 * c + i, 0:1]
    put_hidden(1)

    for k in range(K):
        hid_sends[k].wait_send()
        for r in (xrs[k], xag[k], yrs[k], yag[k]):
            r.drain()
        remote(seven(st1, k), seven(st1, k), STAT1, k, cy(1)).wait_send()
        remote(seven(st3, k), seven(st3, k), STAT2, k, z_dev(1)).wait_send()
        remote(theirs.at[k], arrive.at[k], PAIRSUM, k, partner).wait_send()
        remote(seven(zin, k), seven(zin, k), ZSUM, k, z_dev(1)).wait_send()
        span = fin.at[k, y, :, pl.ds(0, 7 * COL8)]
        remote(span, span, ZOUT, k, z_dev(1)).wait_send()
        span3 = divs.at[k, pl.ds(0, 3)]
        remote(span3, span3, DIV, k, x_dev(lax.rem(w + 1, 4))).wait_send()
        for i in range(4):
            pltpu.make_async_copy(
                fin.at[k, i], ghid_ref.at[pl.ds(k * PAIR + i * TOK4, TOK4)], out_sem.at[k, i]
            ).wait()
    for j in range(8):
        cols = slice(j * 256, (j + 1) * 256)
        pltpu.make_async_copy(gout.at[:, cols], gh_ref.at[:, cols], out_sem.at[2, j]).wait()

    @pl.when(holder)
    def _():
        for _, there in tea_copies:
            there.wait_send()


def body(hidden, head, teacher):
    head_t = head.reshape(WID, REAL).T
    teacher_t = jnp.transpose(teacher, (1, 2, 0))
    any_space = pl.BlockSpec(memory_space=pl.ANY)
    vmem = pltpu.VMEM
    div, gh, ghid = pl.pallas_call(
        kernel,
        out_shape=(
            jax.ShapeDtypeStruct((4, BLK), F32),
            jax.ShapeDtypeStruct((REAL, WID), BF16),
            jax.ShapeDtypeStruct((K * PAIR, WID), BF16),
        ),
        in_specs=[any_space] * 3,
        out_specs=(pl.BlockSpec(memory_space=pltpu.VMEM), any_space, any_space),
        scratch_shapes=[
            vmem((K, 2, PAIR, WID), BF16),
            vmem((REAL, WID), BF16),
            vmem((K, REAL, BLK), BF16),
            vmem((K, 4, ROWS, BLK), WIRE),
            vmem((K, 2, HALF, BLK), WIRE),
            vmem((K, 2, ROWS, BLK), WIRE),
            vmem((K, REAL, BLK), F32),
            vmem((K, 8, BLK), F32),
            vmem((K, 8, 8, BLK), F32),
            vmem((K, 8, BLK), F32),
            vmem((K, 8, 8, BLK), F32),
            vmem((K, 4, ROWS, BLK), BF16),
            vmem((PAIR, ROWS), BF16),
            vmem((K, PAIR, WID), BF16),
            vmem((K, PAIR, WID), BF16),
            vmem((PAIR, WID), F32),
            vmem((K, 4, TOK4, WID), BF16),
            vmem((K, 2, TOK4 // 2, WID), BF16),
            vmem((K, 2, TOK4, WID), BF16),
            vmem((K, 8, TOK4, COL8), BF16),
            vmem((K, 8, TOK4, COL8), BF16),
            vmem((K, 4, TOK4, WID), BF16),
            vmem((REAL, WID), BF16),
            vmem((K, 4, 8, BLK), F32),
            pltpu.SemaphoreType.DMA((K, NSEM)),
            pltpu.SemaphoreType.DMA((K, NSEM)),
            pltpu.SemaphoreType.DMA((K, 2)),
            pltpu.SemaphoreType.DMA((1,)),
            pltpu.SemaphoreType.DMA((3, 8)),
        ],
        compiler_params=pltpu.CompilerParams(
            collective_id=0, has_side_effects=True, vmem_limit_bytes=60 * 1024 * 1024
        ),
    )(hidden, head_t, teacher_t)
    return div.reshape(K * PAIR), gh.T.reshape(WID, 1, REAL), ghid


def solution(mesh):
    return jax.shard_map(
        body,
        mesh=mesh,
        in_specs=(P("dp", "width"), P("width", "dp", "vocab"), P("dp", None, "vocab")),
        out_specs=(P("dp"), P("width", "dp", "vocab"), P("dp", "width")),
        check_vma=False,
    )
```

```python
import jax
import jax.numpy as jnp
from jax import lax
from jax.experimental import pallas as pl
from jax.experimental.pallas import tpu as pltpu
from jax.sharding import PartitionSpec as P

VOCAB = 64128
MESH = pl.DeviceIdType.MESH
BF16, F32 = jnp.bfloat16, jnp.float32
WIRE = F32
K = 2
ROWS, REAL = 1008, 1002
BLK = 128
PAIR = 2 * BLK
CHUNK = 2 * PAIR
WID = 2048
HALF = 512
TOK4 = PAIR // 4
PARTS = 2 * K
WID2 = WID // 2
COL8 = WID2 // 8

HID, TEA, STAT1, STAT2, PAIRSUM, ZSUM, ZOUT = range(7)
XRS, XAG, YRS, YAG = 7, 13, 17, 23
DIV = 27
NSEM = 28
LHID, LTEA, LOUT = range(3)


class Ring4:
    def __init__(self, axis, pos, device, send, recv):
        self.p = pos
        self.right = device(lax.rem(pos + 1, 4))
        self.left = device(lax.rem(pos + 3, 4))
        self.send, self.recv = send, recv

    def copy(self, src, dst, n, k, peer):
        return pltpu.make_async_remote_copy(
            src_ref=src, dst_ref=dst, send_sem=self.send.at[k, n], recv_sem=self.recv.at[k, n],
            device_id=peer, device_id_type=MESH,
        )


class ReduceScatter4(Ring4):
    def setup(self, k, base, src, first, second, half):
        p = self.p
        nxt, opp, prv = lax.rem(p + 1, 4), lax.rem(p + 2, 4), lax.rem(p + 3, 4)
        rows = src.shape[2]
        a, b = pl.ds(0, half), pl.ds(half, rows - half)
        self.c1 = [
            self.copy(src.at[k, opp, a], first.at[k, 0, a], base + 0, k, self.right),
            self.copy(src.at[k, opp, b], first.at[k, 1, pl.ds(0, rows - half)], base + 1, k, self.left),
        ]
        self.c2 = [
            self.copy(src.at[k, nxt, b], second.at[k, 0, b], base + 2, k, self.right),
            self.copy(src.at[k, prv, a], second.at[k, 1, a], base + 3, k, self.left),
        ]
        self.c3 = [
            self.copy(first.at[k, 0, a], second.at[k, 0, a], base + 4, k, self.right),
            self.copy(first.at[k, 1, pl.ds(0, rows - half)], second.at[k, 1, b], base + 5, k, self.left),
        ]
        self.args = (k, src, first, half, rows, nxt, prv)
        return self

    def start1(self):
        for c in self.c1:
            c.start()

    def start2(self):
        for c in self.c2:
            c.start()

    def relay(self):
        k, src, first, half, rows, nxt, prv = self.args
        self.c1[0].wait_recv()
        s = first[k, 0, 0:half].astype(F32) + src[k, nxt, 0:half].astype(F32)
        first[k, 0, 0:half] = s.astype(first.dtype)
        self.c3[0].start()
        self.c1[1].wait_recv()
        s = first[k, 1, 0 : rows - half].astype(F32) + src[k, prv, half:rows].astype(F32)
        first[k, 1, 0 : rows - half] = s.astype(first.dtype)
        self.c3[1].start()

    def finish(self):
        for c in self.c2 + self.c3:
            c.wait_recv()

    def drain(self):
        for c in self.c1 + self.c2 + self.c3:
            c.wait_send()


class AllGather4(Ring4):
    def setup(self, k, base, buf, half):
        p = self.p
        nxt, prv = lax.rem(p + 1, 4), lax.rem(p + 3, 4)
        rows = buf.shape[2]
        a, b = pl.ds(0, half), pl.ds(half, rows - half)
        self.c1 = [
            self.copy(buf.at[k, p], buf.at[k, p], base + 0, k, self.right),
            self.copy(buf.at[k, p], buf.at[k, p], base + 1, k, self.left),
        ]
        self.c2 = [
            self.copy(buf.at[k, prv, a], buf.at[k, prv, a], base + 2, k, self.right),
            self.copy(buf.at[k, nxt, b], buf.at[k, nxt, b], base + 3, k, self.left),
        ]
        return self

    def start1(self):
        for c in self.c1:
            c.start()

    def relay(self):
        self.c1[0].wait_recv()
        self.c2[0].start()
        self.c1[1].wait_recv()
        self.c2[1].start()

    def finish(self):
        for c in self.c2:
            c.wait_recv()

    def drain(self):
        for c in self.c1 + self.c2:
            c.wait_send()


def merge(tiles):
    ms = [t[0:1] for t in tiles]
    mt = [t[2:3] for t in tiles]
    top_s, top_t = ms[0], mt[0]
    for i in range(1, len(tiles)):
        top_s, top_t = jnp.maximum(top_s, ms[i]), jnp.maximum(top_t, mt[i])
    sum_s = sum_t = cross = jnp.zeros_like(top_s)
    for t, a, b in zip(tiles, ms, mt):
        fs, ft = jnp.exp(a - top_s), jnp.exp(b - top_t)
        sum_s = sum_s + t[1:2] * fs
        sum_t = sum_t + t[3:4] * ft
        cross = cross + t[4:5] * ft
    return top_s, sum_s, top_t, sum_t, cross


def kernel(
    hid_ref, head_ref, tea_ref, div_ref, gh_ref, ghid_ref,
    hid, head, tea, part, first, second, logit, st0, st1, st2, st3, grad, gradn,
    theirs, arrive, mine, ysrc, yfirst, ysecond, zsrc, zin, fin, gout, divs,
    send, recv, local, head_sem, out_sem,
):
    c = lax.axis_index("dp")
    w = lax.axis_index("width")
    v = lax.axis_index("vocab")
    y, z = lax.rem(v, 4), v // 4
    partner = {"dp": 1 - c}

    def x_dev(q):
        return {"width": q}

    def y_dev(q):
        return {"vocab": z * 4 + q}

    def cy(i):
        j = lax.rem(c * 4 + y + i, 8)
        return {"dp": j // 4, "vocab": z * 4 + lax.rem(j, 4)}

    def z_dev(i):
        return {"vocab": lax.rem(z + i, 8) * 4 + y}

    head_copy = pltpu.make_async_copy(head_ref, head, head_sem.at[0])
    head_copy.start()
    hid_copies = [
        pltpu.make_async_copy(hid_ref.at[pl.ds(k * PAIR, PAIR)], hid.at[k, c], local.at[k, LHID]) for k in range(K)
    ]
    for cp in hid_copies:
        cp.start()

    barrier = pltpu.get_barrier_semaphore()
    for i in range(1, 8):
        pl.semaphore_signal(barrier, inc=1, device_id=cy(i), device_id_type=MESH)
        pl.semaphore_signal(barrier, inc=1, device_id=z_dev(i), device_id_type=MESH)
    for i in range(1, 4):
        pl.semaphore_signal(barrier, inc=1, device_id=x_dev(lax.rem(w + i, 4)), device_id_type=MESH)
    pl.semaphore_wait(barrier, 17)

    def remote(src, dst, n, k, peer):
        return pltpu.make_async_remote_copy(
            src_ref=src, dst_ref=dst, send_sem=send.at[k, n], recv_sem=recv.at[k, n],
            device_id=peer, device_id_type=MESH,
        )

    hid_sends = [remote(hid_ref.at[pl.ds(k * PAIR, PAIR)], hid.at[k, c], HID, k, partner) for k in range(K)]
    for cp in hid_sends:
        cp.start()
    holder = c == w // 2
    place = lax.rem(w, 2) * BLK

    def tea_copy(k):
        cols = pl.ds(pl.multiple_of(k * PAIR + place, BLK), BLK)
        return (
            pltpu.make_async_copy(tea_ref.at[c, :, cols], tea.at[k], local.at[k, LTEA]),
            remote(tea_ref.at[1 - c, :, cols], tea.at[k], TEA, k, partner),
        )

    tea_copies = [tea_copy(k) for k in range(K)]

    @pl.when(holder)
    def _():
        for here, there in tea_copies:
            there.start()
            here.start()

    xrs = [ReduceScatter4("width", w, x_dev, send, recv).setup(k, XRS, part, first, second, HALF) for k in range(K)]
    xag = [AllGather4("width", w, x_dev, send, recv).setup(k, XAG, grad, HALF) for k in range(K)]
    yrs = [
        ReduceScatter4("vocab", y, y_dev, send, recv).setup(k, YRS, ysrc, yfirst, ysecond, TOK4 // 2) for k in range(PARTS)
    ]
    yag = [AllGather4("vocab", y, y_dev, send, recv).setup(k, YAG, fin, TOK4 // 2) for k in range(PARTS)]

    def logits(k, d):
        for lo, hi in ((0, HALF), (HALF, REAL)):
            if hi == REAL:
                part[k, 2 * d, ROWS - 8 : ROWS] = jnp.zeros((8, BLK), WIRE)
                part[k, 2 * d + 1, ROWS - 8 : ROWS] = jnp.zeros((8, BLK), WIRE)
            out = lax.dot_general(
                head[lo:hi, :], hid[k, d], (((1,), (1,)), ((), ())), preferred_element_type=F32
            )
            part[k, 2 * d, lo:hi] = out[:, :BLK].astype(WIRE)
            part[k, 2 * d + 1, lo:hi] = out[:, BLK:].astype(WIRE)

    def wait_hidden(k):
        hid_copies[k].wait()
        hid_sends[k].wait_recv()

    def statistics(k):
        xrs[k].finish()

        @pl.when(holder)
        def _():
            tea_copies[k][0].wait()

        @pl.when(jnp.logical_not(holder))
        def _():
            tea_copies[k][1].wait_recv()

        x = part[k, w, 0:REAL] + second[k, 0, 0:REAL] + second[k, 1, 0:REAL]
        logit[k] = x
        t = tea[k].astype(F32)
        top_s = jnp.max(x, axis=0, keepdims=True)
        top_t = jnp.max(t, axis=0, keepdims=True)
        exp_t = jnp.exp(t - top_t)
        st0[k, 0:1] = top_s
        st0[k, 1:2] = jnp.sum(jnp.exp(x - top_s), axis=0, keepdims=True)
        st0[k, 2:3] = top_t
        st0[k, 3:4] = jnp.sum(exp_t, axis=0, keepdims=True)
        st0[k, 4:5] = jnp.sum(exp_t * (t - x), axis=0, keepdims=True)
        st0[k, 5:8] = jnp.zeros((3, BLK), F32)
        me = c * 4 + y
        st1[k, me] = st0[k]
        for i in range(1, 8):
            remote(st0.at[k], st1.at[k, me], STAT1, k, cy(i)).start()

    def seven(buf, k):
        return buf.at[k, pl.ds(0, 7)]

    def statistics_far(k):
        remote(seven(st1, k), seven(st1, k), STAT1, k, cy(1)).wait_recv()
        got = merge([st1[k, i] for i in range(8)])
        for i in range(5):
            st2[k, i : i + 1] = got[i]
        st2[k, 5:8] = jnp.zeros((3, BLK), F32)
        st3[k, z] = st2[k]
        for i in range(1, 8):
            remote(st2.at[k], st3.at[k, z], STAT2, k, z_dev(i)).start()

    def gradient(k):
        remote(seven(st3, k), seven(st3, k), STAT2, k, z_dev(1)).wait_recv()
        top_s, sum_s, top_t, sum_t, cross = merge([st3[k, i] for i in range(8)])
        lse_s = top_s + jnp.log(sum_s)
        lse_t = top_t + jnp.log(sum_t)
        divs[k, w] = jnp.broadcast_to(cross / sum_t - lse_t + lse_s, (8, BLK))
        g = VOCAB * (jnp.exp(logit[k] - lse_s) - jnp.exp(tea[k].astype(F32) - lse_t))
        grad[k, w, ROWS - 16 : ROWS] = jnp.zeros((16, BLK), BF16)
        grad[k, w, 0:REAL] = g.astype(BF16)
        xag[k].start1()
        for i in range(1, 4):
            remote(divs.at[k, w], divs.at[k, w], DIV, k, x_dev(lax.rem(w + i, 4))).start()

    def hidden_terms(k):
        xag[k].finish()
        for d, final in ((1 - c, False), (c, True)):
            gn = jnp.concatenate([grad[k, 2 * d], grad[k, 2 * d + 1]], axis=1)
            gradn[...] = gn.T

            for half in range(2):
                n = 2 * k + half

                def tile(j, carry):
                    here = pl.ds(pl.multiple_of(j * 512, 512), 512)
                    cols = pl.ds(pl.multiple_of(half * WID2 + j * 512, 512), 512)
                    out = jnp.dot(gradn[:, 0:REAL], head[:, cols], preferred_element_type=F32)
                    if final:
                        mine[:, cols] = out
                    else:
                        theirs[n, :, here] = out.astype(BF16)
                    return carry

                lax.fori_loop(0, WID2 // 512, tile, 0)
                if not final:
                    remote(theirs.at[n], arrive.at[n], PAIRSUM, n, partner).start()

    def pair_sum(k):
        for half in range(2):
            n = 2 * k + half
            remote(theirs.at[n], arrive.at[n], PAIRSUM, n, partner).wait_recv()
            cols = slice(half * WID2, (half + 1) * WID2)
            for i in range(4):
                rows = slice(i * TOK4, (i + 1) * TOK4)
                ysrc[n, i] = (mine[rows, cols] + arrive[n, rows].astype(F32)).astype(BF16)
            yrs[n].start1()
            yrs[n].start2()

    def z_sum(k):
        yrs[k].finish()
        s = ysrc[k, y].astype(F32) + ysecond[k, 0].astype(F32) + ysecond[k, 1].astype(F32)
        s = s.astype(BF16)
        for i in range(8):
            zsrc[k, i] = s[:, i * COL8 : (i + 1) * COL8]
        zin[k, z] = zsrc[k, z]
        for i in range(1, 8):
            q = lax.rem(z + i, 8)
            remote(zsrc.at[k, q], zin.at[k, z], ZSUM, k, z_dev(i)).start()

    def my_cols():
        return pl.ds(pl.multiple_of(z * COL8, COL8), COL8)

    def z_gather(k):
        remote(seven(zin, k), seven(zin, k), ZSUM, k, z_dev(1)).wait_recv()
        s = zin[k, 0].astype(F32)
        for i in range(1, 8):
            s = s + zin[k, i].astype(F32)
        fin[k, y, :, my_cols()] = s.astype(BF16)
        mine_ref = fin.at[k, y, :, my_cols()]
        for i in range(1, 8):
            remote(mine_ref, mine_ref, ZOUT, k, z_dev(i)).start()

    def y_gather(k):
        span = fin.at[k, y, :, pl.ds(0, 7 * COL8)]
        remote(span, span, ZOUT, k, z_dev(1)).wait_recv()
        yag[k].start1()

    def out_copy(n, i):
        rows = pl.ds(n // 2 * PAIR + i * TOK4, TOK4)
        cols = pl.ds(n % 2 * WID2, WID2)
        return pltpu.make_async_copy(fin.at[n, i], ghid_ref.at[rows, cols], out_sem.at[n, i])

    def put_hidden(n):
        yag[n].finish()
        for i in range(4):
            out_copy(n, i).start()

    def head_terms(js):
        for j in js:
            cols = slice(j * 256, (j + 1) * 256)
            for lo, hi in ((0, HALF), (HALF, REAL)):
                total = None
                for k in range(K):
                    g = jnp.concatenate([grad[k, b, lo:hi] for b in range(4)], axis=1)
                    h = hid[k, :, :, cols].reshape(CHUNK, 256)
                    term = jnp.dot(g, h, preferred_element_type=F32)
                    total = term if total is None else total + term
                gout[lo:hi, cols] = total.astype(BF16)
            pltpu.make_async_copy(gout.at[:, cols], gh_ref.at[:, cols], out_sem.at[PARTS, j]).start()

    opp, own = 1 - w // 2, w // 2
    wait_hidden(0)
    head_copy.wait()
    logits(0, opp)
    xrs[0].start1()
    logits(0, own)
    xrs[0].start2()
    wait_hidden(1)
    logits(1, opp)
    logits(1, own)
    xrs[0].relay()
    xrs[1].start1()
    xrs[1].start2()
    statistics(0)
    xrs[1].relay()
    statistics_far(0)
    gradient(0)
    statistics(1)
    xag[0].relay()
    statistics_far(1)
    hidden_terms(0)
    gradient(1)
    pair_sum(0)
    xag[1].relay()
    yrs[0].relay()
    yrs[1].relay()
    z_sum(0)
    z_sum(1)
    hidden_terms(1)
    z_gather(0)
    z_gather(1)
    pair_sum(1)
    y_gather(0)
    y_gather(1)
    head_terms((0,))
    yrs[2].relay()
    head_terms((1,))
    yrs[3].relay()
    yag[0].relay()
    yag[1].relay()
    z_sum(2)
    head_terms((2,))
    z_sum(3)
    put_hidden(0)
    put_hidden(1)
    head_terms((3,))
    z_gather(2)
    head_terms((4,))
    z_gather(3)
    y_gather(2)
    head_terms((5,))
    y_gather(3)
    head_terms((6,))
    yag[2].relay()
    head_terms((7,))
    yag[3].relay()
    for k in range(K):
        span3 = divs.at[k, pl.ds(0, 3)]
        remote(span3, span3, DIV, k, x_dev(lax.rem(w + 1, 4))).wait_recv()
        for i in range(2):
            div_ref[2 * k + i : 2 * k + i + 1] = divs[k, 2 * c + i, 0:1]
    put_hidden(2)
    put_hidden(3)

    for k in range(K):
        hid_sends[k].wait_send()
        for r in (xrs[k], xag[k]):
            r.drain()
        remote(seven(st1, k), seven(st1, k), STAT1, k, cy(1)).wait_send()
        remote(seven(st3, k), seven(st3, k), STAT2, k, z_dev(1)).wait_send()
        span3 = divs.at[k, pl.ds(0, 3)]
        remote(span3, span3, DIV, k, x_dev(lax.rem(w + 1, 4))).wait_send()
    for n in range(PARTS):
        for r in (yrs[n], yag[n]):
            r.drain()
        remote(theirs.at[n], arrive.at[n], PAIRSUM, n, partner).wait_send()
        remote(seven(zin, n), seven(zin, n), ZSUM, n, z_dev(1)).wait_send()
        span = fin.at[n, y, :, pl.ds(0, 7 * COL8)]
        remote(span, span, ZOUT, n, z_dev(1)).wait_send()
        for i in range(4):
            out_copy(n, i).wait()
    for j in range(8):
        cols = slice(j * 256, (j + 1) * 256)
        pltpu.make_async_copy(gout.at[:, cols], gh_ref.at[:, cols], out_sem.at[PARTS, j]).wait()

    @pl.when(holder)
    def _():
        for _, there in tea_copies:
            there.wait_send()


def body(hidden, head, teacher):
    head_t = head.reshape(WID, REAL).T
    teacher_t = jnp.transpose(teacher, (1, 2, 0))
    any_space = pl.BlockSpec(memory_space=pl.ANY)
    vmem = pltpu.VMEM
    div, gh, ghid = pl.pallas_call(
        kernel,
        out_shape=(
            jax.ShapeDtypeStruct((4, BLK), F32),
            jax.ShapeDtypeStruct((REAL, WID), BF16),
            jax.ShapeDtypeStruct((K * PAIR, WID), BF16),
        ),
        in_specs=[any_space] * 3,
        out_specs=(pl.BlockSpec(memory_space=pltpu.VMEM), any_space, any_space),
        scratch_shapes=[
            vmem((K, 2, PAIR, WID), BF16),
            vmem((REAL, WID), BF16),
            vmem((K, REAL, BLK), BF16),
            vmem((K, 4, ROWS, BLK), WIRE),
            vmem((K, 2, HALF, BLK), WIRE),
            vmem((K, 2, ROWS, BLK), WIRE),
            vmem((K, REAL, BLK), F32),
            vmem((K, 8, BLK), F32),
            vmem((K, 8, 8, BLK), F32),
            vmem((K, 8, BLK), F32),
            vmem((K, 8, 8, BLK), F32),
            vmem((K, 4, ROWS, BLK), BF16),
            vmem((PAIR, ROWS), BF16),
            vmem((PARTS, PAIR, WID2), BF16),
            vmem((PARTS, PAIR, WID2), BF16),
            vmem((PAIR, WID), F32),
            vmem((PARTS, 4, TOK4, WID2), BF16),
            vmem((PARTS, 2, TOK4 // 2, WID2), BF16),
            vmem((PARTS, 2, TOK4, WID2), BF16),
            vmem((PARTS, 8, TOK4, COL8), BF16),
            vmem((PARTS, 8, TOK4, COL8), BF16),
            vmem((PARTS, 4, TOK4, WID2), BF16),
            vmem((REAL, WID), BF16),
            vmem((K, 4, 8, BLK), F32),
            pltpu.SemaphoreType.DMA((PARTS, NSEM)),
            pltpu.SemaphoreType.DMA((PARTS, NSEM)),
            pltpu.SemaphoreType.DMA((K, 2)),
            pltpu.SemaphoreType.DMA((1,)),
            pltpu.SemaphoreType.DMA((PARTS + 1, 8)),
        ],
        compiler_params=pltpu.CompilerParams(
            collective_id=0, has_side_effects=True, vmem_limit_bytes=60 * 1024 * 1024
        ),
    )(hidden, head_t, teacher_t)
    return div.reshape(K * PAIR), gh.T.reshape(WID, 1, REAL), ghid


def solution(mesh):
    return jax.shard_map(
        body,
        mesh=mesh,
        in_specs=(P("dp", "width"), P("width", "dp", "vocab"), P("dp", None, "vocab")),
        out_specs=(P("dp"), P("width", "dp", "vocab"), P("dp", "width")),
        check_vma=False,
    )
```
